32 devices in a mesh: strip: 4 (over z), cross: 8 (over y, x, core).
Axes of the slice: x: 2, y: 2, z: 4, core: 2. Of those that a mesh axis runs over, the one named last changes fastest.
Arguments:
- rhs: bfloat16 [4, 64, 14336], P('strip', None, 'cross'), may hold values from -6 to 6
- inverse: bfloat16 [4, 8, 1792, 1792], P('strip', 'cross'), may hold values from -2 to 2
- dis_fwd: bfloat16 [4, 8, 256, 1792], P('strip', 'cross'), may hold values from -0.1875 to 0.1875
- agg_fwd: bfloat16 [4, 14336, 256], P('strip', 'cross'), may hold values from -0.0625 to 0.0625
- phase_fwd: float32 [4, 128], P('strip'), may hold values from -3.140625 to 3.140625
- gain_fwd: float32 [4, 128], P('strip'), may hold values from 0.5 to 1
- dis_back: bfloat16 [4, 8, 256, 1792], P('strip', 'cross'), may hold values from -0.1875 to 0.1875
- agg_back: bfloat16 [4, 14336, 256], P('strip', 'cross'), may hold values from -0.0625 to 0.0625
- phase_back: float32 [4, 128], P('strip'), may hold values from -3.140625 to 3.140625
- gain_back: float32 [4, 128], P('strip'), may hold values from 0.5 to 1
Outputs:
- first_pass: float32 [4, 64, 14336], P('strip', None, 'cross')
- solution: float32 [4, 64, 14336], P('strip', None, 'cross')
The draws below stay inside these ranges and needn't reach their ends.
All inputs are finite; a program needn't handle non-finite values.
Results may differ from the reference program's by a relative error of at most 0.04.
Values may be sent and summed in bfloat16 or wider, within the bound.
A program may use at most 64 MiB of HBM per device.

```python
import math
import jax
import jax.numpy as jnp
from jax import lax

UNK = 1792
MODES = 256
HALF = 128
ANGLES = 64
STRIPS = 4
CLUSTERS = 8
ROW = 14336


def draw_inverse(key, part):
    diag_key = jax.random.fold_in(key, 11)
    off_key = jax.random.fold_in(key, 12)
    diag_scale = jax.random.uniform(diag_key, (STRIPS, CLUSTERS, UNK), jnp.float32, 0.5, 1.5)
    spread = jnp.clip(jax.random.normal(off_key, (STRIPS, CLUSTERS, UNK, UNK), jnp.float32), -4.0, 4.0) * (0.5 / UNK ** 0.5)
    identity = jnp.eye(UNK, dtype=jnp.float32)
    return (spread + identity * diag_scale[..., None]).astype(jnp.bfloat16)


def with_spikes(drawn, stream_key, source, target, blocks, factor):
    owner, partner = [(jnp.arange(drawn.shape[dim]) // (drawn.shape[dim] // blocks)).reshape([-1 if axis == dim else 1 for axis in range(drawn.ndim)]) for dim in (source, target)]
    chosen = jax.random.permutation(stream_key, blocks)[partner]
    strong = (owner == chosen) | (owner == (partner + blocks // 2) % blocks)
    return jnp.where(strong, factor * drawn, drawn)


def levels(own_key, shape, shards, low, largest):
    def one(axis_at, parts):
        draws = jax.random.uniform(jax.random.fold_in(jax.random.fold_in(own_key, 6), axis_at), (parts,), jnp.float32, low / len(shards), largest / len(shards))
        return jnp.repeat(jnp.exp(draws), shape[axis_at] // parts).reshape((-1,) + (1,) * (len(shape) - axis_at - 1))

    level = one(*shards[0])
    for cut in shards[1:]:
        level = level * one(*cut)
    return level


def noise(stream_key, dims, scale, reach, pieces=(), kind=jnp.bfloat16):
    result = jax.random.normal(stream_key, dims, jnp.float32) * scale
    if len(pieces) > 0:
        result = levels(stream_key, dims, pieces, -0.22, 0.18) * result
    return jnp.clip(result, min=-reach, max=reach).astype(kind)


def heavy_noise(own_key, dims, width, most, cuts, heavy, kind=jnp.bfloat16):
    values = width * jax.random.normal(own_key, dims, jnp.float32)
    if cuts:
        values = values * levels(own_key, dims, cuts, -0.22, 0.18)
    return jnp.clip(with_spikes(values, jax.random.fold_in(own_key, 3), *heavy), -most, most).astype(kind)


def setup_inputs(seed: int = 0) -> dict:
    key_list = jax.random.split(jax.random.key(seed), 11)
    return {
        "rhs": noise(key_list[0], (STRIPS, ANGLES, ROW), 1.0, 6.0, ((0, 4), (2, 8))),
        "inverse": draw_inverse(jax.random.fold_in(key_list[10], 71), 0),
        "dis_fwd": noise(key_list[2], (STRIPS, CLUSTERS, MODES, UNK), (0.5 * MODES ** -0.5), 0.1875, ((0, 4), (1, 8))),
        "agg_fwd": heavy_noise(key_list[3], (STRIPS, ROW, MODES), ROW ** -0.5, 0.0625, ((0, 4), (1, 8)), (1, 2, 8, 2.0)),
        "phase_fwd": jnp.clip(jax.random.uniform(key_list[4], (STRIPS, HALF), jnp.float32, -3.140625, 3.140625), -3.140625, 3.140625),
        "gain_fwd": jnp.clip(jnp.exp(math.log(1.0) - 0.6931472 * jax.random.uniform(key_list[5], (STRIPS, HALF), jnp.float32) ** levels(key_list[5], (STRIPS, HALF), ((0, 4),), -0.2, 0.2)), 0.5, 1.0),
        "dis_back": noise(key_list[6], (STRIPS, CLUSTERS, MODES, UNK), (0.5 * MODES ** -0.5), 0.1875, ((0, 4), (1, 8))),
        "agg_back": heavy_noise(key_list[7], (STRIPS, ROW, MODES), ROW ** -0.5, 0.0625, ((0, 4), (1, 8)), (1, 2, 8, 2.0)),
        "phase_back": jnp.clip(jax.random.uniform(key_list[8], (STRIPS, HALF), jnp.float32, -3.140625, 3.140625), -3.140625, 3.140625),
        "gain_back": jnp.clip(jnp.exp(math.log(1.0) - 0.6931472 * jax.random.uniform(key_list[9], (STRIPS, HALF), jnp.float32) ** levels(key_list[9], (STRIPS, HALF), ((0, 4),), -0.2, 0.2)), 0.5, 1.0),
    }


def rotate(carry, phase, gain):
    half = phase.shape[0]
    real_part = carry[:, :half]
    imag_part = carry[:, half:]
    cosine = jnp.cos(phase)
    sine = jnp.sin(phase)
    return jnp.concatenate([gain * (cosine * real_part - sine * imag_part), gain * (sine * real_part + cosine * imag_part)], axis=1)


def rounded(value):
    return lax.optimization_barrier(value.astype(jnp.bfloat16)).astype(jnp.float32)


def strip_solve(source, carried, inv_strip, dis_strip, agg_strip):
    angles, row = source.shape
    clusters, unk = inv_strip.shape[0], inv_strip.shape[1]
    spread = jnp.einsum("am,cmu->acu", rounded(carried), dis_strip.astype(jnp.float32), precision=lax.Precision.HIGHEST).reshape(angles, row)
    field = source - spread
    answer = jnp.einsum("acv,cvu->acu", rounded(field).reshape(angles, clusters, unk), inv_strip.astype(jnp.float32), precision=lax.Precision.HIGHEST).reshape(angles, row)
    summed = jnp.dot(answer.astype(jnp.bfloat16), agg_strip, preferred_element_type=jnp.float32)
    return field, answer, summed


def reference(rhs, inverse, dis_fwd, agg_fwd, phase_fwd, gain_fwd, dis_back, agg_back, phase_back, gain_back):
    strips, angles, row = rhs.shape
    modes = dis_fwd.shape[2]
    carry = jnp.zeros((angles, modes), jnp.float32)
    fields = []
    firsts = []
    for strip in range(strips):
        field, answer, summed = strip_solve(rhs[strip].astype(jnp.float32), carry, inverse[strip], dis_fwd[strip], agg_fwd[strip])
        fields.append(field)
        firsts.append(answer)
        carry = rotate(carry, phase_fwd[strip], gain_fwd[strip]) + summed
    carry = jnp.zeros((angles, modes), jnp.float32)
    seconds = [None] * strips
    for strip in range(strips - 1, -1, -1):
        field, answer, summed = strip_solve(fields[strip], carry, inverse[strip], dis_back[strip], agg_back[strip])
        seconds[strip] = answer
        carry = rotate(carry, phase_back[strip], gain_back[strip]) + summed
    return jnp.stack(firsts), jnp.stack(seconds)
```

```python
import functools

import jax
import jax.numpy as jnp
from jax import lax
from jax.experimental import pallas as pl
from jax.experimental.pallas import tpu as pltpu
from jax.sharding import PartitionSpec as P

MESH = pl.DeviceIdType.MESH
BF = jnp.bfloat16
F32 = jnp.float32
T_RS, B_RS, T_AG, N_RS, N_AG, E_RS, C_ON, D_ON = range(8)


def dot(a, b):
    return jnp.dot(a, b, preferred_element_type=F32)


def kernel(
    strips, n, width,
    rhs, inverse, dis_fwd, agg_fwd, phase_fwd, gain_fwd, dis_back, agg_back, phase_back, gain_back,
    first_ref, second_ref,
    x_f, x_b, inv, agg_f, agg_b, p, u_f, u_b,
    t_own, t_out, t_in, n_own, n_out, n_in, t_all, n_all,
    b_own, b_out, b_in, e_own, e_out, e_in, b_red, e_red,
    c_out, c_all, d_out, d_all,
    load_sem, sems,
):
    s = lax.axis_index("strip")
    me = lax.axis_index("cross")
    is_first = s == 0
    is_last = s == strips - 1
    inner = jnp.logical_and(s > 0, s < strips - 1)
    angles = rhs.shape[1]
    modes = agg_f.shape[1]
    half = modes // 2
    unk = p.shape[1]
    blocks = unk // width
    rows = angles // n

    loads = [
        pltpu.make_async_copy(rhs.at[0], x_f.at[pl.ds(0, angles)], load_sem.at[0]),
        pltpu.make_async_copy(dis_fwd.at[0, 0], x_f.at[pl.ds(angles, modes)], load_sem.at[1]),
        pltpu.make_async_copy(agg_fwd.at[0], agg_f, load_sem.at[2]),
        pltpu.make_async_copy(dis_back.at[0, 0], x_b, load_sem.at[3]),
        pltpu.make_async_copy(agg_back.at[0], agg_b, load_sem.at[4]),
    ]
    inv_loads = [
        pltpu.make_async_copy(
            inverse.at[0, 0, :, pl.ds(j * width, width)], inv.at[j], load_sem.at[5 + j]
        )
        for j in range(blocks)
    ]
    loads[0].start()
    loads[1].start()
    for copy in inv_loads:
        copy.start()
    for copy in loads[2:]:
        copy.start()

    barrier = pltpu.get_barrier_semaphore()

    def greet(strip, peer):
        pl.semaphore_signal(barrier, inc=1, device_id=(strip, peer), device_id_type=MESH)

    def others(fn):
        def step(j, carry):
            fn(lax.rem(me + j, n))
            return carry
        lax.fori_loop(1, n, step, 0)

    def everyone(fn):
        def step(j, carry):
            fn(lax.rem(me + j, n))
            return carry
        lax.fori_loop(0, n, step, 0)

    others(lambda peer: greet(s, peer))

    @pl.when(s > 0)
    def _():
        everyone(lambda peer: greet(s - 1, peer))

    @pl.when(s < strips - 1)
    def _():
        everyone(lambda peer: greet(s + 1, peer))

    def remote(kind, src, dst, strip, peer):
        return pltpu.make_async_remote_copy(
            src_ref=src,
            dst_ref=dst,
            send_sem=sems.at[kind, 0, peer],
            recv_sem=sems.at[kind, 1, me],
            device_id=(strip, peer),
            device_id_type=MESH,
        )

    def arrived(kind, dst, peer):
        pltpu.make_async_remote_copy(
            src_ref=dst.at[peer],
            dst_ref=dst.at[peer],
            send_sem=sems.at[kind, 0, peer],
            recv_sem=sems.at[kind, 1, peer],
            device_id=(s, peer),
            device_id_type=MESH,
        ).wait_recv()

    def scatter(kind, out, into):
        others(lambda peer: remote(kind, out.at[peer], into.at[me], s, peer).start())

    def scatter_sent(kind, out, into):
        others(lambda peer: remote(kind, out.at[peer], into.at[me], s, peer).wait_send())

    def total(kind, own, into):
        others(lambda peer: arrived(kind, into, peer))
        value = own[me]
        for j in range(1, n):
            value = value + into[lax.rem(me + j, n)].astype(F32)
        return value

    def share(kind, buf):
        others(lambda peer: remote(kind, buf.at[me], buf.at[me], s, peer).start())

    def share_sent(kind, buf):
        others(lambda peer: remote(kind, buf.at[me], buf.at[me], s, peer).wait_send())

    def pass_on(kind, src, buf, strip):
        everyone(lambda peer: remote(kind, src, buf.at[me], strip, peer).start())

    def passed_on(kind, src, buf, strip):
        everyone(lambda peer: remote(kind, src, buf.at[me], strip, peer).wait_send())

    def split(value, own, out):
        part = value.shape[0] // n
        for k in range(n):
            piece = value[k * part:(k + 1) * part]
            own[k] = piece
            out[k] = piece.astype(BF)

    def joined(buf):
        return jnp.concatenate([buf[k] for k in range(n)], axis=0)

    def rotated(value, phase, gain):
        real, imag = value[:, :half], value[:, half:]
        cosine, sine, g = jnp.cos(phase[...]), jnp.sin(phase[...]), gain[...]
        return jnp.concatenate(
            [g * (cosine * real - sine * imag), g * (sine * real + cosine * imag)], axis=1
        )

    loads[0].wait()
    loads[1].wait()
    for j in range(blocks):
        inv_loads[j].wait()
        product = dot(x_f[...], inv[j])
        p[:, j * width:(j + 1) * width] = product[:angles]
        u_f[:, j * width:(j + 1) * width] = product[angles:].astype(BF)
    loads[2].wait()

    @pl.when(inner)
    def _():
        split(dot(u_f[...], agg_f[...]), t_own, t_out)

    @pl.when(s < strips - 1)
    def _():
        split(dot(p[...].astype(BF), agg_f[...]), b_own, b_out)

    greeted = (n - 1) + jnp.where(s > 0, n, 0) + jnp.where(s < strips - 1, n, 0)
    pl.semaphore_wait(barrier, greeted)

    @pl.when(s < strips - 1)
    def _():
        scatter(B_RS, b_out, b_in)

    @pl.when(inner)
    def _():
        scatter(T_RS, t_out, t_in)

    loads[3].wait()
    loads[4].wait()

    @pl.when(is_last)
    def _():
        split(dot(p[...].astype(BF), agg_b[...]), e_own, e_out)
        scatter(E_RS, e_out, e_in)
        split(dot(u_f[...], agg_b[...]), n_own, n_out)

    @pl.when(s < strips - 1)
    def _():
        for j in range(blocks):
            u_b[:, j * width:(j + 1) * width] = dot(x_b[...], inv[j]).astype(BF)

    @pl.when(inner)
    def _():
        split(dot(u_b[...], agg_b[...]), n_own, n_out)

    @pl.when(s < strips - 1)
    def _():
        b_red[...] = total(B_RS, b_own, b_in)

    @pl.when(is_first)
    def _():
        c_out[...] = b_red[...].astype(BF)
        pass_on(C_ON, c_out, c_all, s + 1)

    @pl.when(inner)
    def _():
        t_all[me] = total(T_RS, t_own, t_in).astype(BF)
        share(T_AG, t_all)

    @pl.when(s > 0)
    def _():
        scatter(N_RS, n_out, n_in)

    @pl.when(inner)
    def _():
        others(lambda peer: arrived(T_AG, t_all, peer))
        arrived(C_ON, c_all, me)
        held = c_all[me]
        leaving = rotated(held.astype(F32), phase_fwd, gain_fwd) + b_red[...]
        leaving = leaving - dot(held, joined(t_all))
        c_out[...] = leaving.astype(BF)
        pass_on(C_ON, c_out, c_all, s + 1)

    @pl.when(s > 0)
    def _():
        n_all[me] = total(N_RS, n_own, n_in).astype(BF)
        share(N_AG, n_all)

    @pl.when(is_last)
    def _():
        e_red[...] = total(E_RS, e_own, e_in)
        others(lambda peer: arrived(N_AG, n_all, peer))
        arrived(C_ON, c_all, me)
        d_out[...] = (e_red[...] - dot(c_all[me], joined(n_all))).astype(BF)
        pass_on(D_ON, d_out, d_all, s - 1)

    @pl.when(is_first)
    def _():
        first_ref[0] = p[...]

    @pl.when(s > 0)
    def _():
        others(lambda peer: arrived(C_ON, c_all, peer))
        first_ref[0] = p[...] - dot(joined(c_all), u_f[...])

    @pl.when(inner)
    def _():
        split(dot(first_ref[0].astype(BF), agg_b[...]), e_own, e_out)
        scatter(E_RS, e_out, e_in)
        others(lambda peer: arrived(N_AG, n_all, peer))
        e_red[...] = total(E_RS, e_own, e_in)
        arrived(D_ON, d_all, me)
        held = d_all[me]
        leaving = rotated(held.astype(F32), phase_back, gain_back) + e_red[...]
        leaving = leaving - dot(held, joined(n_all))
        d_out[...] = leaving.astype(BF)
        pass_on(D_ON, d_out, d_all, s - 1)

    @pl.when(is_last)
    def _():
        second_ref[0] = first_ref[0]

    @pl.when(is_first)
    def _():
        arrived(D_ON, d_all, me)

    @pl.when(s < strips - 1)
    def _():
        others(lambda peer: arrived(D_ON, d_all, peer))
        second_ref[0] = first_ref[0] - dot(joined(d_all), u_b[...])

    @pl.when(inner)
    def _():
        scatter_sent(T_RS, t_out, t_in)
        share_sent(T_AG, t_all)

    @pl.when(s < strips - 1)
    def _():
        scatter_sent(B_RS, b_out, b_in)
        passed_on(C_ON, c_out, c_all, s + 1)

    @pl.when(s > 0)
    def _():
        scatter_sent(N_RS, n_out, n_in)
        share_sent(N_AG, n_all)
        scatter_sent(E_RS, e_out, e_in)
        passed_on(D_ON, d_out, d_all, s - 1)


def body(strips, n, rhs, inverse, dis_fwd, agg_fwd, phase_fwd, gain_fwd, dis_back, agg_back, phase_back, gain_back):
    _, angles, unk = rhs.shape
    modes = agg_fwd.shape[2]
    width = 256 if unk % 256 == 0 else unk
    blocks = unk // width
    rows, part = angles // n, modes // n
    hbm = pl.BlockSpec(memory_space=pl.ANY)
    vmem = pl.BlockSpec(memory_space=pltpu.VMEM)
    out = jax.ShapeDtypeStruct((1, angles, unk), F32)
    return pl.pallas_call(
        functools.partial(kernel, strips, n, width),
        out_shape=(out, out),
        in_specs=[hbm, hbm, hbm, hbm, vmem, vmem, hbm, hbm, vmem, vmem],
        out_specs=(vmem, vmem),
        scratch_shapes=[
            pltpu.VMEM((angles + modes, unk), BF),
            pltpu.VMEM((modes, unk), BF),
            pltpu.VMEM((blocks, unk, width), BF),
            pltpu.VMEM((unk, modes), BF),
            pltpu.VMEM((unk, modes), BF),
            pltpu.VMEM((angles, unk), F32),
            pltpu.VMEM((modes, unk), BF),
            pltpu.VMEM((modes, unk), BF),
        ]
        + [pltpu.VMEM((n, part, modes), kind) for kind in (F32, BF, BF) * 2 + (BF, BF)]
        + [pltpu.VMEM((n, rows, modes), kind) for kind in (F32, BF, BF) * 2]
        + [pltpu.VMEM((rows, modes), F32)] * 2
        + [pltpu.VMEM((rows, modes), BF), pltpu.VMEM((n, rows, modes), BF)] * 2
        + [pltpu.SemaphoreType.DMA((5 + blocks,)), pltpu.SemaphoreType.DMA((8, 2, n))],
        compiler_params=pltpu.CompilerParams(
            collective_id=0, has_side_effects=True, vmem_limit_bytes=60 * 1024 * 1024
        ),
    )(rhs, inverse, dis_fwd, agg_fwd, phase_fwd, gain_fwd, dis_back, agg_back, phase_back, gain_back)


def solution(mesh):
    strips, n = mesh.shape["strip"], mesh.shape["cross"]
    return jax.shard_map(
        functools.partial(body, strips, n),
        mesh=mesh,
        in_specs=(
            P("strip", None, "cross"),
            P("strip", "cross", None, None),
            P("strip", "cross", None, None),
            P("strip", "cross", None),
            P("strip", None),
            P("strip", None),
            P("strip", "cross", None, None),
            P("strip", "cross", None),
            P("strip", None),
            P("strip", None),
        ),
        out_specs=(P("strip", None, "cross"), P("strip", None, "cross")),
        check_vma=False,
    )
```

```python
import functools

import jax
import jax.numpy as jnp
from jax import lax
from jax.experimental import pallas as pl
from jax.experimental.pallas import tpu as pltpu
from jax.sharding import PartitionSpec as P

MESH = pl.DeviceIdType.MESH
BF = jnp.bfloat16
F32 = jnp.float32
KINDS = 11
T_RS, B_RS, T_AG, N_RS, N_AG, E_RS, C_IN, C_ON, C_SH, D_ON, D_SH = range(KINDS)


def dot(a, b):
    return jnp.dot(a, b, preferred_element_type=F32)


def kernel(
    strips, n, width,
    rhs, inverse, dis_fwd, agg_fwd, phase_fwd, gain_fwd, dis_back, agg_back, phase_back, gain_back,
    first_ref, second_ref,
    x_f, x_b, inv, agg_f, agg_b, p, u_f, u_b,
    t_own, t_out, t_in, n_own, n_out, n_in, t_all, n_all,
    b_own, b_out, b_in, e_own, e_out, e_in, c_in, b_red, e_red,
    c_out, c_all, d_out, d_all,
    turns, coef, load_sem, sems,
):
    s = lax.axis_index("strip")
    me = lax.axis_index("cross")
    is_first = s == 0
    is_last = s == strips - 1
    inner = jnp.logical_and(s > 0, s < strips - 1)
    angles = rhs.shape[1]
    modes = agg_f.shape[1]
    half = modes // 2
    unk = p.shape[1]
    blocks = unk // width
    rows = angles // n

    loads = [
        pltpu.make_async_copy(rhs.at[0], x_f.at[pl.ds(0, angles)], load_sem.at[0]),
        pltpu.make_async_copy(dis_fwd.at[0, 0], x_f.at[pl.ds(angles, modes)], load_sem.at[1]),
        pltpu.make_async_copy(agg_fwd.at[0], agg_f, load_sem.at[2]),
        pltpu.make_async_copy(dis_back.at[0, 0], x_b, load_sem.at[3]),
        pltpu.make_async_copy(agg_back.at[0], agg_b, load_sem.at[4]),
    ]
    inv_loads = [
        pltpu.make_async_copy(
            inverse.at[0, 0, :, pl.ds(j * width, width)], inv.at[j], load_sem.at[5 + j]
        )
        for j in range(blocks)
    ]
    turn_loads = [
        pltpu.make_async_copy(ref, turns.at[j], load_sem.at[5 + blocks + j])
        for j, ref in enumerate((phase_fwd, gain_fwd, phase_back, gain_back))
    ]
    loads[0].start()
    loads[1].start()
    for copy in inv_loads:
        copy.start()
    loads[2].start()

    barrier = pltpu.get_barrier_semaphore()

    def greet(strip, peer):
        pl.semaphore_signal(barrier, inc=1, device_id=(strip, peer), device_id_type=MESH)

    def others(fn):
        def step(j, carry):
            fn(lax.rem(me + j, n))
            return carry
        lax.fori_loop(1, n, step, 0)

    def everyone(fn):
        def step(j, carry):
            fn(lax.rem(me + j, n))
            return carry
        lax.fori_loop(0, n, step, 0)

    others(lambda peer: greet(s, peer))

    @pl.when(s > 0)
    def _():
        everyone(lambda peer: greet(s - 1, peer))

    @pl.when(s < strips - 1)
    def _():
        everyone(lambda peer: greet(s + 1, peer))

    def remote(kind, src, dst, strip, peer):
        return pltpu.make_async_remote_copy(
            src_ref=src,
            dst_ref=dst,
            send_sem=sems.at[kind, 0, peer],
            recv_sem=sems.at[kind, 1, me],
            device_id=(strip, peer),
            device_id_type=MESH,
        )

    def arrived(kind, dst, peer):
        pltpu.make_async_remote_copy(
            src_ref=dst.at[peer],
            dst_ref=dst.at[peer],
            send_sem=sems.at[kind, 0, peer],
            recv_sem=sems.at[kind, 1, peer],
            device_id=(s, peer),
            device_id_type=MESH,
        ).wait_recv()

    def scatter(kind, out, into):
        others(lambda peer: remote(kind, out.at[peer], into.at[me], s, peer).start())

    def scatter_sent(kind, out, into):
        others(lambda peer: remote(kind, out.at[peer], into.at[me], s, peer).wait_send())

    def total(kind, own, into):
        others(lambda peer: arrived(kind, into, peer))
        value = own[me]
        for j in range(1, n):
            value = value + into[lax.rem(me + j, n)].astype(F32)
        return value

    def share(kind, buf):
        others(lambda peer: remote(kind, buf.at[me], buf.at[me], s, peer).start())

    def share_sent(kind, buf):
        others(lambda peer: remote(kind, buf.at[me], buf.at[me], s, peer).wait_send())

    def split(value, own, out):
        part = value.shape[0] // n
        for k in range(n):
            piece = value[k * part:(k + 1) * part]
            own[k] = piece
            out[k] = piece.astype(BF)

    def joined(buf):
        return jnp.concatenate([buf[k] for k in range(n)], axis=0)

    def rotated(value, at):
        real, imag = value[:, :half], value[:, half:]
        cosine, sine = coef[at], coef[at + 1]
        return jnp.concatenate(
            [cosine * real - sine * imag, sine * real + cosine * imag], axis=1
        )

    loads[0].wait()
    loads[1].wait()

    @pl.when(is_first)
    def _():
        for j in range(blocks):
            inv_loads[j].wait()
            p[:, j * width:(j + 1) * width] = dot(x_f[:angles], inv[j])

    @pl.when(s > 0)
    def _():
        for j in range(blocks):
            inv_loads[j].wait()
            product = dot(x_f[...], inv[j])
            p[:, j * width:(j + 1) * width] = product[:angles]
            u_f[:, j * width:(j + 1) * width] = product[angles:].astype(BF)

    for copy in loads[3:] + turn_loads:
        copy.start()
    loads[2].wait()

    @pl.when(inner)
    def _():
        split(dot(u_f[...], agg_f[...]), t_own, t_out)

    @pl.when(is_first)
    def _():
        split(dot(p[...].astype(BF), agg_f[...]), b_own, b_out)

    greeted = (n - 1) + jnp.where(s > 0, n, 0) + jnp.where(s < strips - 1, n, 0)
    pl.semaphore_wait(barrier, greeted)

    @pl.when(is_first)
    def _():
        everyone(lambda peer: remote(C_IN, b_out.at[peer], c_in.at[me], s + 1, peer).start())

    @pl.when(inner)
    def _():
        scatter(T_RS, t_out, t_in)
        split(dot(p[...].astype(BF), agg_f[...]), b_own, b_out)
        scatter(B_RS, b_out, b_in)

    loads[3].wait()
    loads[4].wait()
    for copy in turn_loads:
        copy.wait()
    for at in (0, 2):
        coef[at] = jnp.cos(turns[at]) * turns[at + 1]
        coef[at + 1] = jnp.sin(turns[at]) * turns[at + 1]

    @pl.when(is_last)
    def _():
        split(dot(p[...].astype(BF), agg_b[...]), e_own, e_out)
        scatter(E_RS, e_out, e_in)
        split(dot(u_f[...], agg_b[...]), n_own, n_out)

    @pl.when(s < strips - 1)
    def _():
        for j in range(blocks):
            u_b[:, j * width:(j + 1) * width] = dot(x_b[...], inv[j]).astype(BF)

    @pl.when(inner)
    def _():
        split(dot(u_b[...], agg_b[...]), n_own, n_out)

    @pl.when(inner)
    def _():
        t_all[me] = total(T_RS, t_own, t_in).astype(BF)
        share(T_AG, t_all)
        b_red[...] = total(B_RS, b_own, b_in)

    @pl.when(s > 0)
    def _():
        scatter(N_RS, n_out, n_in)

    def take_carry():
        @pl.when(s == 1)
        def _():
            everyone(lambda peer: arrived(C_IN, c_in, peer))
            value = c_in[0].astype(F32)
            for j in range(1, n):
                value = value + c_in[j].astype(F32)
            c_all[me] = value.astype(BF)

        @pl.when(s > 1)
        def _():
            arrived(C_ON, c_all, me)

    @pl.when(inner)
    def _():
        others(lambda peer: arrived(T_AG, t_all, peer))
        matrix = joined(t_all)
        take_carry()
        held = c_all[me]
        leaving = rotated(held.astype(F32), 0) + b_red[...]
        c_out[...] = (leaving - dot(held, matrix)).astype(BF)
        remote(C_ON, c_out, c_all.at[me], s + 1, me).start()
        share(C_SH, c_all)

    @pl.when(s > 0)
    def _():
        n_all[me] = total(N_RS, n_own, n_in).astype(BF)
        share(N_AG, n_all)

    @pl.when(is_last)
    def _():
        e_red[...] = total(E_RS, e_own, e_in)
        others(lambda peer: arrived(N_AG, n_all, peer))
        matrix = joined(n_all)
        take_carry()
        d_out[...] = (e_red[...] - dot(c_all[me], matrix)).astype(BF)

    def send_back():
        @pl.when(s == 1)
        def _():
            everyone(lambda peer: remote(D_ON, d_out, d_all.at[me], s - 1, peer).start())

        @pl.when(s > 1)
        def _():
            remote(D_ON, d_out, d_all.at[me], s - 1, me).start()

    @pl.when(is_last)
    def _():
        send_back()
        share(C_SH, c_all)

    @pl.when(is_first)
    def _():
        first_ref[0] = p[...]

    @pl.when(s > 0)
    def _():
        others(lambda peer: arrived(C_SH, c_all, peer))
        first_ref[0] = p[...] - dot(joined(c_all), u_f[...])

    @pl.when(inner)
    def _():
        split(dot(first_ref[0].astype(BF), agg_b[...]), e_own, e_out)
        scatter(E_RS, e_out, e_in)
        others(lambda peer: arrived(N_AG, n_all, peer))
        e_red[...] = total(E_RS, e_own, e_in)
        matrix = joined(n_all)
        arrived(D_ON, d_all, me)
        held = d_all[me]
        leaving = rotated(held.astype(F32), 2) + e_red[...]
        d_out[...] = (leaving - dot(held, matrix)).astype(BF)
        send_back()
        share(D_SH, d_all)

    @pl.when(is_last)
    def _():
        second_ref[0] = first_ref[0]

    @pl.when(is_first)
    def _():
        everyone(lambda peer: arrived(D_ON, d_all, peer))

    @pl.when(inner)
    def _():
        others(lambda peer: arrived(D_SH, d_all, peer))

    @pl.when(s < strips - 1)
    def _():
        second_ref[0] = first_ref[0] - dot(joined(d_all), u_b[...])

    @pl.when(is_first)
    def _():
        everyone(lambda peer: remote(C_IN, b_out.at[peer], c_in.at[me], s + 1, peer).wait_send())

    @pl.when(inner)
    def _():
        scatter_sent(T_RS, t_out, t_in)
        share_sent(T_AG, t_all)
        scatter_sent(B_RS, b_out, b_in)
        remote(C_ON, c_out, c_all.at[me], s + 1, me).wait_send()
        share_sent(D_SH, d_all)

    @pl.when(s > 0)
    def _():
        share_sent(C_SH, c_all)
        scatter_sent(N_RS, n_out, n_in)
        share_sent(N_AG, n_all)
        scatter_sent(E_RS, e_out, e_in)

    @pl.when(s == 1)
    def _():
        everyone(lambda peer: remote(D_ON, d_out, d_all.at[me], s - 1, peer).wait_send())

    @pl.when(s > 1)
    def _():
        remote(D_ON, d_out, d_all.at[me], s - 1, me).wait_send()


def body(strips, n, rhs, inverse, dis_fwd, agg_fwd, phase_fwd, gain_fwd, dis_back, agg_back, phase_back, gain_back):
    _, angles, unk = rhs.shape
    modes = agg_fwd.shape[2]
    width = 256 if unk % 256 == 0 else unk
    blocks = unk // width
    rows, part = angles // n, modes // n
    hbm = pl.BlockSpec(memory_space=pl.ANY)
    vmem = pl.BlockSpec(memory_space=pltpu.VMEM)
    out = pltpu.VMEM((1, angles, unk), F32)
    return pl.pallas_call(
        functools.partial(kernel, strips, n, width),
        out_shape=(out, out),
        in_specs=[hbm] * 10,
        out_specs=(vmem, vmem),
        scratch_shapes=[
            pltpu.VMEM((angles + modes, unk), BF),
            pltpu.VMEM((modes, unk), BF),
            pltpu.VMEM((blocks, unk, width), BF),
            pltpu.VMEM((unk, modes), BF),
            pltpu.VMEM((unk, modes), BF),
            pltpu.VMEM((angles, unk), F32),
            pltpu.VMEM((modes, unk), BF),
            pltpu.VMEM((modes, unk), BF),
        ]
        + [pltpu.VMEM((n, part, modes), kind) for kind in (F32, BF, BF) * 2 + (BF, BF)]
        + [pltpu.VMEM((n, rows, modes), kind) for kind in (F32, BF, BF) * 2 + (BF,)]
        + [pltpu.VMEM((rows, modes), F32)] * 2
        + [pltpu.VMEM((rows, modes), BF), pltpu.VMEM((n, rows, modes), BF)] * 2
        + [pltpu.VMEM((4, 1, modes // 2), F32)] * 2
        + [pltpu.SemaphoreType.DMA((9 + blocks,)), pltpu.SemaphoreType.DMA((KINDS, 2, n))],
        compiler_params=pltpu.CompilerParams(
            collective_id=0, has_side_effects=True, vmem_limit_bytes=60 * 1024 * 1024
        ),
    )(rhs, inverse, dis_fwd, agg_fwd, phase_fwd, gain_fwd, dis_back, agg_back, phase_back, gain_back)


def solution(mesh):
    strips, n = mesh.shape["strip"], mesh.shape["cross"]
    return jax.shard_map(
        functools.partial(body, strips, n),
        mesh=mesh,
        in_specs=(
            P("strip", None, "cross"),
            P("strip", "cross", None, None),
            P("strip", "cross", None, None),
            P("strip", "cross", None),
            P("strip", None),
            P("strip", None),
            P("strip", "cross", None, None),
            P("strip", "cross", None),
            P("strip", None),
            P("strip", None),
        ),
        out_specs=(P("strip", None, "cross"), P("strip", None, "cross")),
        check_vma=False,
    )
```

```python
import functools

import jax
import jax.numpy as jnp
from jax import lax
from jax.experimental import pallas as pl
from jax.experimental.pallas import tpu as pltpu
from jax.sharding import PartitionSpec as P

MESH = pl.DeviceIdType.MESH
BF = jnp.bfloat16
F32 = jnp.float32
KINDS = 11
T_RS, B_RS, T_AG, N_RS, N_AG, E_RS, C_IN, C_ON, C_SH, D_ON, D_SH = range(KINDS)


def dot(a, b):
    return jnp.dot(a, b, preferred_element_type=F32)


def kernel(
    strips, n, width,
    rhs, inverse, dis_fwd, agg_fwd, phase_fwd, gain_fwd, dis_back, agg_back, phase_back, gain_back,
    first_ref, second_ref,
    x_f, x_b, inv, agg_f, agg_b, p, u_f, u_b,
    t_own, t_out, t_in, n_own, n_out, n_in, t_all, n_all,
    b_own, b_out, b_in, e_own, e_out, e_in, c_in, b_red, e_red,
    c_out, c_all, d_out, d_all,
    turns, coef, load_sem, sems,
):
    s = lax.axis_index("strip")
    me = lax.axis_index("cross")
    is_first = s == 0
    is_last = s == strips - 1
    inner = jnp.logical_and(s > 0, s < strips - 1)
    angles = rhs.shape[1]
    modes = agg_f.shape[1]
    half = modes // 2
    unk = p.shape[1]
    blocks = unk // width
    rows = angles // n

    load_rhs = pltpu.make_async_copy(rhs.at[0], x_b.at[pl.ds(0, angles)], load_sem.at[0])
    load_dis = pltpu.make_async_copy(dis_fwd.at[0, 0], x_f, load_sem.at[1])
    load_agg = pltpu.make_async_copy(agg_fwd.at[0], agg_f, load_sem.at[2])
    load_last = pltpu.make_async_copy(agg_back.at[0], agg_f, load_sem.at[2])
    load_dis_b = pltpu.make_async_copy(
        dis_back.at[0, 0], x_b.at[pl.ds(angles, modes)], load_sem.at[3]
    )
    load_agg_b = pltpu.make_async_copy(agg_back.at[0], agg_b, load_sem.at[4])
    inv_loads = [
        pltpu.make_async_copy(
            inverse.at[0, 0, :, pl.ds(j * width, width)], inv.at[j], load_sem.at[5 + j]
        )
        for j in range(blocks)
    ]
    turn_loads = [
        pltpu.make_async_copy(ref, turns.at[j], load_sem.at[5 + blocks + j])
        for j, ref in enumerate((phase_fwd, gain_fwd, phase_back, gain_back))
    ]
    @pl.when(is_first)
    def _():
        load_rhs.start()

    @pl.when(s > 0)
    def _():
        load_dis.start()

    @pl.when(is_last)
    def _():
        load_last.start()

    @pl.when(s < strips - 1)
    def _():
        load_agg.start()

    for copy in inv_loads:
        copy.start()

    @pl.when(s > 0)
    def _():
        load_rhs.start()

    @pl.when(s < strips - 1)
    def _():
        load_dis_b.start()

    @pl.when(inner)
    def _():
        load_agg_b.start()

    for copy in turn_loads:
        copy.start()

    barrier = pltpu.get_barrier_semaphore()

    def greet(strip, peer):
        pl.semaphore_signal(barrier, inc=1, device_id=(strip, peer), device_id_type=MESH)

    def others(fn):
        def step(j, carry):
            fn(lax.rem(me + j, n))
            return carry
        lax.fori_loop(1, n, step, 0)

    def everyone(fn):
        def step(j, carry):
            fn(lax.rem(me + j, n))
            return carry
        lax.fori_loop(0, n, step, 0)

    others(lambda peer: greet(s, peer))

    @pl.when(s > 0)
    def _():
        everyone(lambda peer: greet(s - 1, peer))

    @pl.when(s < strips - 1)
    def _():
        everyone(lambda peer: greet(s + 1, peer))

    def remote(kind, src, dst, strip, peer):
        return pltpu.make_async_remote_copy(
            src_ref=src,
            dst_ref=dst,
            send_sem=sems.at[kind, 0, peer],
            recv_sem=sems.at[kind, 1, me],
            device_id=(strip, peer),
            device_id_type=MESH,
        )

    def arrived(kind, dst, peer):
        pltpu.make_async_remote_copy(
            src_ref=dst.at[peer],
            dst_ref=dst.at[peer],
            send_sem=sems.at[kind, 0, peer],
            recv_sem=sems.at[kind, 1, peer],
            device_id=(s, peer),
            device_id_type=MESH,
        ).wait_recv()

    def scatter(kind, out, into):
        others(lambda peer: remote(kind, out.at[peer], into.at[me], s, peer).start())

    def scatter_sent(kind, out, into):
        others(lambda peer: remote(kind, out.at[peer], into.at[me], s, peer).wait_send())

    def total(kind, own, into):
        others(lambda peer: arrived(kind, into, peer))
        value = own[me]
        for j in range(1, n):
            value = value + into[lax.rem(me + j, n)].astype(F32)
        return value

    def share(kind, buf):
        others(lambda peer: remote(kind, buf.at[me], buf.at[me], s, peer).start())

    def share_sent(kind, buf):
        others(lambda peer: remote(kind, buf.at[me], buf.at[me], s, peer).wait_send())

    def split(value, own, out):
        part = value.shape[0] // n
        for k in range(n):
            piece = value[k * part:(k + 1) * part]
            own[k] = piece
            out[k] = piece.astype(BF)

    def joined(buf):
        return jnp.concatenate([buf[k] for k in range(n)], axis=0)

    def rotated(value, at):
        real, imag = value[:, :half], value[:, half:]
        cosine, sine = coef[at], coef[at + 1]
        return jnp.concatenate(
            [cosine * real - sine * imag, sine * real + cosine * imag], axis=1
        )

    def columns(j):
        return slice(j * width, (j + 1) * width)

    load_agg.wait()

    @pl.when(is_first)
    def _():
        load_rhs.wait()
        value = None
        for j in range(blocks):
            inv_loads[j].wait()
            product = dot(x_b[:angles], inv[j])
            p[:, columns(j)] = product
            term = dot(product.astype(BF), agg_f[columns(j)])
            value = term if value is None else value + term
        split(value, b_own, b_out)

    @pl.when(s > 0)
    def _():
        load_dis.wait()
        for j in range(blocks):
            inv_loads[j].wait()
            product = dot(x_f[...], inv[j]).astype(BF)
            u_f[:, columns(j)] = product
            term = dot(product, agg_f[columns(j)]).reshape(t_own.shape)
            if j == 0:
                t_own[...] = term
            else:
                t_own[...] += term
        t_out[...] = t_own[...].astype(BF)

    greeted = (n - 1) + jnp.where(s > 0, n, 0) + jnp.where(s < strips - 1, n, 0)
    pl.semaphore_wait(barrier, greeted)

    @pl.when(is_first)
    def _():
        everyone(lambda peer: remote(C_IN, b_out.at[peer], c_in.at[me], s + 1, peer).start())

    @pl.when(s > 0)
    def _():
        scatter(T_RS, t_out, t_in)
        load_rhs.wait()
        value = None
        for j in range(blocks):
            product = dot(x_b[:angles], inv[j])
            p[:, columns(j)] = product
            term = dot(product.astype(BF), agg_f[columns(j)])
            value = term if value is None else value + term
        split(value, b_own, b_out)
        scatter(B_RS, b_out, b_in)

    for copy in turn_loads:
        copy.wait()
    for at in (0, 2):
        coef[at] = jnp.cos(turns[at]) * turns[at + 1]
        coef[at + 1] = jnp.sin(turns[at]) * turns[at + 1]

    @pl.when(is_first)
    def _():
        load_dis_b.wait()
        for j in range(blocks):
            u_b[:, columns(j)] = dot(x_b[angles:], inv[j]).astype(BF)

    @pl.when(inner)
    def _():
        load_dis_b.wait()
        load_agg_b.wait()
        for j in range(blocks):
            product = dot(x_b[angles:], inv[j]).astype(BF)
            u_b[:, columns(j)] = product
            term = dot(product, agg_b[columns(j)]).reshape(n_own.shape)
            if j == 0:
                n_own[...] = term
            else:
                n_own[...] += term
        n_out[...] = n_own[...].astype(BF)

    @pl.when(s > 0)
    def _():
        t_all[me] = total(T_RS, t_own, t_in).astype(BF)
        share(T_AG, t_all)
        b_red[...] = total(B_RS, b_own, b_in)

    @pl.when(inner)
    def _():
        scatter(N_RS, n_out, n_in)

    def take_carry():
        @pl.when(s == 1)
        def _():
            everyone(lambda peer: arrived(C_IN, c_in, peer))
            value = c_in[0].astype(F32)
            for j in range(1, n):
                value = value + c_in[j].astype(F32)
            c_all[me] = value.astype(BF)

        @pl.when(s > 1)
        def _():
            arrived(C_ON, c_all, me)

    @pl.when(inner)
    def _():
        others(lambda peer: arrived(T_AG, t_all, peer))
        matrix = joined(t_all)
        take_carry()
        held = c_all[me]
        leaving = rotated(held.astype(F32), 0) + b_red[...]
        c_out[...] = (leaving - dot(held, matrix)).astype(BF)
        remote(C_ON, c_out, c_all.at[me], s + 1, me).start()
        share(C_SH, c_all)

    @pl.when(inner)
    def _():
        n_all[me] = total(N_RS, n_own, n_in).astype(BF)
        share(N_AG, n_all)

    @pl.when(is_last)
    def _():
        others(lambda peer: arrived(T_AG, t_all, peer))
        matrix = joined(t_all)
        take_carry()
        d_out[...] = (b_red[...] - dot(c_all[me], matrix)).astype(BF)

    def send_back():
        @pl.when(s == 1)
        def _():
            everyone(lambda peer: remote(D_ON, d_out, d_all.at[me], s - 1, peer).start())

        @pl.when(s > 1)
        def _():
            remote(D_ON, d_out, d_all.at[me], s - 1, me).start()

    @pl.when(is_last)
    def _():
        send_back()
        share(C_SH, c_all)

    @pl.when(is_first)
    def _():
        first_ref[0] = p[...]

    @pl.when(s > 0)
    def _():
        others(lambda peer: arrived(C_SH, c_all, peer))
        first_ref[0] = p[...] - dot(joined(c_all), u_f[...])

    @pl.when(inner)
    def _():
        split(dot(first_ref[0].astype(BF), agg_b[...]), e_own, e_out)
        scatter(E_RS, e_out, e_in)
        others(lambda peer: arrived(N_AG, n_all, peer))
        e_red[...] = total(E_RS, e_own, e_in)
        matrix = joined(n_all)
        arrived(D_ON, d_all, me)
        held = d_all[me]
        leaving = rotated(held.astype(F32), 2) + e_red[...]
        d_out[...] = (leaving - dot(held, matrix)).astype(BF)
        send_back()
        share(D_SH, d_all)

    @pl.when(is_last)
    def _():
        second_ref[0] = first_ref[0]

    @pl.when(is_first)
    def _():
        everyone(lambda peer: arrived(D_ON, d_all, peer))

    @pl.when(inner)
    def _():
        others(lambda peer: arrived(D_SH, d_all, peer))

    @pl.when(s < strips - 1)
    def _():
        second_ref[0] = first_ref[0] - dot(joined(d_all), u_b[...])

    @pl.when(is_first)
    def _():
        everyone(lambda peer: remote(C_IN, b_out.at[peer], c_in.at[me], s + 1, peer).wait_send())

    @pl.when(inner)
    def _():
        scatter_sent(N_RS, n_out, n_in)
        share_sent(N_AG, n_all)
        scatter_sent(E_RS, e_out, e_in)
        remote(C_ON, c_out, c_all.at[me], s + 1, me).wait_send()
        share_sent(D_SH, d_all)

    @pl.when(s > 0)
    def _():
        scatter_sent(T_RS, t_out, t_in)
        share_sent(T_AG, t_all)
        scatter_sent(B_RS, b_out, b_in)
        share_sent(C_SH, c_all)

    @pl.when(s == 1)
    def _():
        everyone(lambda peer: remote(D_ON, d_out, d_all.at[me], s - 1, peer).wait_send())

    @pl.when(s > 1)
    def _():
        remote(D_ON, d_out, d_all.at[me], s - 1, me).wait_send()


def body(strips, n, rhs, inverse, dis_fwd, agg_fwd, phase_fwd, gain_fwd, dis_back, agg_back, phase_back, gain_back):
    _, angles, unk = rhs.shape
    modes = agg_fwd.shape[2]
    width = 256 if unk % 256 == 0 else unk
    blocks = unk // width
    rows, part = angles // n, modes // n
    hbm = pl.BlockSpec(memory_space=pl.ANY)
    vmem = pl.BlockSpec(memory_space=pltpu.VMEM)
    out = pltpu.VMEM((1, angles, unk), F32)
    return pl.pallas_call(
        functools.partial(kernel, strips, n, width),
        out_shape=(out, out),
        in_specs=[hbm] * 10,
        out_specs=(vmem, vmem),
        scratch_shapes=[
            pltpu.VMEM((modes, unk), BF),
            pltpu.VMEM((angles + modes, unk), BF),
            pltpu.VMEM((blocks, unk, width), BF),
            pltpu.VMEM((unk, modes), BF),
            pltpu.VMEM((unk, modes), BF),
            pltpu.VMEM((angles, unk), F32),
            pltpu.VMEM((modes, unk), BF),
            pltpu.VMEM((modes, unk), BF),
        ]
        + [pltpu.VMEM((n, part, modes), kind) for kind in (F32, BF, BF) * 2 + (BF, BF)]
        + [pltpu.VMEM((n, rows, modes), kind) for kind in (F32, BF, BF) * 2 + (BF,)]
        + [pltpu.VMEM((rows, modes), F32)] * 2
        + [pltpu.VMEM((rows, modes), BF), pltpu.VMEM((n, rows, modes), BF)] * 2
        + [pltpu.VMEM((4, 1, modes // 2), F32)] * 2
        + [pltpu.SemaphoreType.DMA((9 + blocks,)), pltpu.SemaphoreType.DMA((KINDS, 2, n))],
        compiler_params=pltpu.CompilerParams(
            collective_id=0, has_side_effects=True, vmem_limit_bytes=60 * 1024 * 1024
        ),
    )(rhs, inverse, dis_fwd, agg_fwd, phase_fwd, gain_fwd, dis_back, agg_back, phase_back, gain_back)


def solution(mesh):
    strips, n = mesh.shape["strip"], mesh.shape["cross"]
    return jax.shard_map(
        functools.partial(body, strips, n),
        mesh=mesh,
        in_specs=(
            P("strip", None, "cross"),
            P("strip", "cross", None, None),
            P("strip", "cross", None, None),
            P("strip", "cross", None),
            P("strip", None),
            P("strip", None),
            P("strip", "cross", None, None),
            P("strip", "cross", None),
            P("strip", None),
            P("strip", None),
        ),
        out_specs=(P("strip", None, "cross"), P("strip", None, "cross")),
        check_vma=False,
    )
```

```python
import functools

import jax
import jax.numpy as jnp
from jax import lax
from jax.experimental import pallas as pl
from jax.experimental.pallas import tpu as pltpu
from jax.sharding import PartitionSpec as P

MESH = pl.DeviceIdType.MESH
BF = jnp.bfloat16
F32 = jnp.float32
KINDS = 11
T_RS, B_RS, T_AG, N_RS, N_AG, E_RS, C_IN, C_ON, C_SH, D_ON, D_SH = range(KINDS)


def dot(a, b):
    return jnp.dot(a, b, preferred_element_type=F32)


def kernel(
    strips, n, width,
    rhs, inverse, dis_fwd, agg_fwd, phase_fwd, gain_fwd, dis_back, agg_back, phase_back, gain_back,
    first_ref, second_ref,
    x_f, x_b, inv, agg_f, agg_b, p, u_f, u_b,
    t_own, t_out, t_in, n_own, n_out, n_in, t_all, n_all,
    b_own, b_out, b_in, e_own, e_out, e_in, c_in, b_red, e_red,
    c_out, c_all, d_out, d_all,
    turns, coef, load_sem, sems,
):
    s = lax.axis_index("strip")
    me = lax.axis_index("cross")
    is_first = s == 0
    is_last = s == strips - 1
    inner = jnp.logical_and(s > 0, s < strips - 1)
    angles = rhs.shape[1]
    modes = agg_f.shape[1]
    half = modes // 2
    unk = p.shape[1]
    blocks = unk // width
    rows = angles // n

    load_rhs = pltpu.make_async_copy(rhs.at[0], x_b.at[pl.ds(0, angles)], load_sem.at[0])
    load_dis = pltpu.make_async_copy(dis_fwd.at[0, 0], x_f, load_sem.at[1])
    load_agg = pltpu.make_async_copy(agg_fwd.at[0], agg_f, load_sem.at[2])
    load_last = pltpu.make_async_copy(agg_back.at[0], agg_f, load_sem.at[2])
    load_dis_b = pltpu.make_async_copy(
        dis_back.at[0, 0], x_b.at[pl.ds(angles, modes)], load_sem.at[3]
    )
    load_agg_b = pltpu.make_async_copy(agg_back.at[0], agg_b, load_sem.at[4])
    inv_loads = [
        pltpu.make_async_copy(
            inverse.at[0, 0, :, pl.ds(j * width, width)], inv.at[j], load_sem.at[5 + j]
        )
        for j in range(blocks)
    ]
    turn_loads = [
        pltpu.make_async_copy(ref, turns.at[j], load_sem.at[5 + blocks + j])
        for j, ref in enumerate((phase_fwd, gain_fwd, phase_back, gain_back))
    ]
    @pl.when(is_first)
    def _():
        load_rhs.start()

    @pl.when(s > 0)
    def _():
        load_dis.start()

    @pl.when(is_last)
    def _():
        load_last.start()

    @pl.when(s < strips - 1)
    def _():
        load_agg.start()

    for copy in inv_loads:
        copy.start()

    @pl.when(s > 0)
    def _():
        load_rhs.start()

    @pl.when(s < strips - 1)
    def _():
        load_dis_b.start()

    @pl.when(inner)
    def _():
        load_agg_b.start()

    for copy in turn_loads:
        copy.start()

    barrier = pltpu.get_barrier_semaphore()

    def greet(strip, peer):
        pl.semaphore_signal(barrier, inc=1, device_id=(strip, peer), device_id_type=MESH)

    def others(fn):
        def step(j, carry):
            fn(lax.rem(me + j, n))
            return carry
        lax.fori_loop(1, n, step, 0)

    def everyone(fn):
        def step(j, carry):
            fn(lax.rem(me + j, n))
            return carry
        lax.fori_loop(0, n, step, 0)

    others(lambda peer: greet(s, peer))

    @pl.when(s > 0)
    def _():
        everyone(lambda peer: greet(s - 1, peer))

    @pl.when(s < strips - 1)
    def _():
        everyone(lambda peer: greet(s + 1, peer))

    def remote(kind, src, dst, strip, peer):
        return pltpu.make_async_remote_copy(
            src_ref=src,
            dst_ref=dst,
            send_sem=sems.at[kind, 0, peer],
            recv_sem=sems.at[kind, 1, me],
            device_id=(strip, peer),
            device_id_type=MESH,
        )

    def arrived(kind, dst, peer):
        pltpu.make_async_remote_copy(
            src_ref=dst.at[peer],
            dst_ref=dst.at[peer],
            send_sem=sems.at[kind, 0, peer],
            recv_sem=sems.at[kind, 1, peer],
            device_id=(s, peer),
            device_id_type=MESH,
        ).wait_recv()

    def scatter(kind, out, into):
        others(lambda peer: remote(kind, out.at[peer], into.at[me], s, peer).start())

    def scatter_sent(kind, out, into):
        others(lambda peer: remote(kind, out.at[peer], into.at[me], s, peer).wait_send())

    def total(kind, own, into):
        others(lambda peer: arrived(kind, into, peer))
        value = own[me]
        for j in range(1, n):
            value = value + into[lax.rem(me + j, n)].astype(F32)
        return value

    def share(kind, buf):
        others(lambda peer: remote(kind, buf.at[me], buf.at[me], s, peer).start())

    def share_sent(kind, buf):
        others(lambda peer: remote(kind, buf.at[me], buf.at[me], s, peer).wait_send())

    def split(value, own, out):
        part = value.shape[0] // n
        for k in range(n):
            piece = value[k * part:(k + 1) * part]
            own[k] = piece
            out[k] = piece.astype(BF)

    def joined(buf):
        return jnp.concatenate([buf[k] for k in range(n)], axis=0)

    def rotated(value, at):
        real, imag = value[:, :half], value[:, half:]
        cosine, sine = coef[at], coef[at + 1]
        return jnp.concatenate(
            [cosine * real - sine * imag, sine * real + cosine * imag], axis=1
        )

    def columns(j):
        return slice(j * width, (j + 1) * width)

    load_agg.wait()

    @pl.when(is_first)
    def _():
        load_rhs.wait()
        value = None
        for j in range(blocks):
            inv_loads[j].wait()
            product = dot(x_b[:angles], inv[j])
            p[:, columns(j)] = product
            term = dot(product.astype(BF), agg_f[columns(j)])
            value = term if value is None else value + term
        split(value, b_own, b_out)

    @pl.when(s > 0)
    def _():
        load_dis.wait()
        for j in range(blocks):
            inv_loads[j].wait()
            product = dot(x_f[...], inv[j]).astype(BF)
            u_f[:, columns(j)] = product
            term = dot(product, agg_f[columns(j)]).reshape(t_own.shape)
            if j == 0:
                t_own[...] = term
            else:
                t_own[...] += term
        t_out[...] = t_own[...].astype(BF)

    greeted = (n - 1) + jnp.where(s > 0, n, 0) + jnp.where(s < strips - 1, n, 0)
    pl.semaphore_wait(barrier, greeted)

    @pl.when(is_first)
    def _():
        everyone(lambda peer: remote(C_IN, b_out.at[peer], c_in.at[me], s + 1, peer).start())

    @pl.when(s > 0)
    def _():
        scatter(T_RS, t_out, t_in)
        load_rhs.wait()
        value = None
        for j in range(blocks):
            product = dot(x_b[:angles], inv[j])
            p[:, columns(j)] = product
            term = dot(product.astype(BF), agg_f[columns(j)])
            value = term if value is None else value + term
        split(value, b_own, b_out)
        scatter(B_RS, b_out, b_in)

    for copy in turn_loads:
        copy.wait()
    for at in (0, 2):
        coef[at] = jnp.cos(turns[at]) * turns[at + 1]
        coef[at + 1] = jnp.sin(turns[at]) * turns[at + 1]

    @pl.when(is_first)
    def _():
        load_dis_b.wait()
        for j in range(blocks):
            u_b[:, columns(j)] = dot(x_b[angles:], inv[j]).astype(BF)

    @pl.when(s > 0)
    def _():
        t_all[me] = total(T_RS, t_own, t_in).astype(BF)
        share(T_AG, t_all)

    @pl.when(inner)
    def _():
        load_dis_b.wait()
        load_agg_b.wait()
        for j in range(blocks):
            product = dot(x_b[angles:], inv[j]).astype(BF)
            u_b[:, columns(j)] = product
            term = dot(product, agg_b[columns(j)]).reshape(n_own.shape)
            if j == 0:
                n_own[...] = term
            else:
                n_own[...] += term
        n_out[...] = n_own[...].astype(BF)

    @pl.when(s > 0)
    def _():
        b_red[...] = total(B_RS, b_own, b_in)

    @pl.when(inner)
    def _():
        scatter(N_RS, n_out, n_in)

    def take_carry():
        @pl.when(s == 1)
        def _():
            everyone(lambda peer: arrived(C_IN, c_in, peer))
            value = c_in[0].astype(F32)
            for j in range(1, n):
                value = value + c_in[j].astype(F32)
            c_all[me] = value.astype(BF)

        @pl.when(s > 1)
        def _():
            arrived(C_ON, c_all, me)

    @pl.when(inner)
    def _():
        others(lambda peer: arrived(T_AG, t_all, peer))
        matrix = joined(t_all)
        take_carry()
        held = c_all[me]
        leaving = rotated(held.astype(F32), 0) + b_red[...]
        c_out[...] = (leaving - dot(held, matrix)).astype(BF)
        remote(C_ON, c_out, c_all.at[me], s + 1, me).start()
        share(C_SH, c_all)

    @pl.when(inner)
    def _():
        n_all[me] = total(N_RS, n_own, n_in).astype(BF)
        share(N_AG, n_all)

    @pl.when(is_last)
    def _():
        others(lambda peer: arrived(T_AG, t_all, peer))
        matrix = joined(t_all)
        take_carry()
        d_out[...] = (b_red[...] - dot(c_all[me], matrix)).astype(BF)

    def send_back():
        @pl.when(s == 1)
        def _():
            everyone(lambda peer: remote(D_ON, d_out, d_all.at[me], s - 1, peer).start())

        @pl.when(s > 1)
        def _():
            remote(D_ON, d_out, d_all.at[me], s - 1, me).start()

    @pl.when(is_last)
    def _():
        send_back()
        share(C_SH, c_all)

    @pl.when(is_first)
    def _():
        first_ref[0] = p[...]

    @pl.when(s > 0)
    def _():
        others(lambda peer: arrived(C_SH, c_all, peer))
        first_ref[0] = p[...] - dot(joined(c_all), u_f[...])

    @pl.when(inner)
    def _():
        split(dot(first_ref[0].astype(BF), agg_b[...]), e_own, e_out)
        scatter(E_RS, e_out, e_in)
        others(lambda peer: arrived(N_AG, n_all, peer))
        e_red[...] = total(E_RS, e_own, e_in)
        matrix = joined(n_all)
        arrived(D_ON, d_all, me)
        held = d_all[me]
        leaving = rotated(held.astype(F32), 2) + e_red[...]
        d_out[...] = (leaving - dot(held, matrix)).astype(BF)
        send_back()
        share(D_SH, d_all)

    @pl.when(is_last)
    def _():
        second_ref[0] = first_ref[0]

    @pl.when(is_first)
    def _():
        everyone(lambda peer: arrived(D_ON, d_all, peer))

    @pl.when(inner)
    def _():
        others(lambda peer: arrived(D_SH, d_all, peer))

    @pl.when(s < strips - 1)
    def _():
        second_ref[0] = first_ref[0] - dot(joined(d_all), u_b[...])

    @pl.when(is_first)
    def _():
        everyone(lambda peer: remote(C_IN, b_out.at[peer], c_in.at[me], s + 1, peer).wait_send())

    @pl.when(inner)
    def _():
        scatter_sent(N_RS, n_out, n_in)
        share_sent(N_AG, n_all)
        scatter_sent(E_RS, e_out, e_in)
        remote(C_ON, c_out, c_all.at[me], s + 1, me).wait_send()
        share_sent(D_SH, d_all)

    @pl.when(s > 0)
    def _():
        scatter_sent(T_RS, t_out, t_in)
        share_sent(T_AG, t_all)
        scatter_sent(B_RS, b_out, b_in)
        share_sent(C_SH, c_all)

    @pl.when(s == 1)
    def _():
        everyone(lambda peer: remote(D_ON, d_out, d_all.at[me], s - 1, peer).wait_send())

    @pl.when(s > 1)
    def _():
        remote(D_ON, d_out, d_all.at[me], s - 1, me).wait_send()


def body(strips, n, rhs, inverse, dis_fwd, agg_fwd, phase_fwd, gain_fwd, dis_back, agg_back, phase_back, gain_back):
    _, angles, unk = rhs.shape
    modes = agg_fwd.shape[2]
    width = 256 if unk % 256 == 0 else unk
    blocks = unk // width
    rows, part = angles // n, modes // n
    hbm = pl.BlockSpec(memory_space=pl.ANY)
    vmem = pl.BlockSpec(memory_space=pltpu.VMEM)
    out = pltpu.VMEM((1, angles, unk), F32)
    return pl.pallas_call(
        functools.partial(kernel, strips, n, width),
        out_shape=(out, out),
        in_specs=[hbm] * 10,
        out_specs=(vmem, vmem),
        scratch_shapes=[
            pltpu.VMEM((modes, unk), BF),
            pltpu.VMEM((angles + modes, unk), BF),
            pltpu.VMEM((blocks, unk, width), BF),
            pltpu.VMEM((unk, modes), BF),
            pltpu.VMEM((unk, modes), BF),
            pltpu.VMEM((angles, unk), F32),
            pltpu.VMEM((modes, unk), BF),
            pltpu.VMEM((modes, unk), BF),
        ]
        + [pltpu.VMEM((n, part, modes), kind) for kind in (F32, BF, BF) * 2 + (BF, BF)]
        + [pltpu.VMEM((n, rows, modes), kind) for kind in (F32, BF, BF) * 2 + (BF,)]
        + [pltpu.VMEM((rows, modes), F32)] * 2
        + [pltpu.VMEM((rows, modes), BF), pltpu.VMEM((n, rows, modes), BF)] * 2
        + [pltpu.VMEM((4, 1, modes // 2), F32)] * 2
        + [pltpu.SemaphoreType.DMA((9 + blocks,)), pltpu.SemaphoreType.DMA((KINDS, 2, n))],
        compiler_params=pltpu.CompilerParams(
            collective_id=0, has_side_effects=True, vmem_limit_bytes=60 * 1024 * 1024
        ),
    )(rhs, inverse, dis_fwd, agg_fwd, phase_fwd, gain_fwd, dis_back, agg_back, phase_back, gain_back)


def solution(mesh):
    strips, n = mesh.shape["strip"], mesh.shape["cross"]
    return jax.shard_map(
        functools.partial(body, strips, n),
        mesh=mesh,
        in_specs=(
            P("strip", None, "cross"),
            P("strip", "cross", None, None),
            P("strip", "cross", None, None),
            P("strip", "cross", None),
            P("strip", None),
            P("strip", None),
            P("strip", "cross", None, None),
            P("strip", "cross", None),
            P("strip", None),
            P("strip", None),
        ),
        out_specs=(P("strip", None, "cross"), P("strip", None, "cross")),
        check_vma=False,
    )
```
